256 devices in a mesh: row: 16 (over y, z_hi), col: 16 (over x, z_lo, core).
Axes of the slice: x: 4, y: 4, z: 8 (z_hi: 4, z_lo: 2; z = z_hi * 2 + z_lo), core: 2. Of those that a mesh axis runs over, the one named last changes fastest.
Arguments:
- features: bfloat16 [65536, 256], P(('col', 'row')), may hold values from -6 to 6
- weight: bfloat16 [256, 256], replicated, may hold values from -0.375 to 0.375
- tile_rows: int32 [16, 16, 320], P('row', 'col'), may hold values from 0 to 31, as said below
- tile_cols: int32 [16, 16, 320], P('row', 'col'), may hold values from 0 to 31
- tile_count: int32 [16, 16], P('row', 'col'), may hold values from 40 to 320, as said below
- tile_values: bfloat16 [16, 16, 320, 128, 128], P('row', 'col'), may hold values from 0.0019989014 to 0.049804688
- grad_out: bfloat16 [65536, 256], P(('row', 'col')), may hold values from -6 to 6
Outputs:
- activations: bfloat16 [65536, 256], P(('row', 'col'))
- feature_grad: bfloat16 [65536, 256], P(('col', 'row'))
- weight_grad: float32 [256, 256], replicated
The draws below stay inside these ranges and needn't reach their ends.
Inputs may be any that keep to these rules, and one draw needn't show every extreme that they name: `tile_rows`: the first tile_count slots of a device name distinct tiles. `tile_count`: slots at or after a device's count are unused and their rows, columns and values are ignored; some device uses all 320 slots in every draw.
All inputs are finite; a program needn't handle non-finite values.
Results may differ from the reference program's by a relative error of at most 0.027.
Values may be sent and summed in bfloat16 or wider, within the bound.
No kernel may reach another device: no remote copies, remote signals or barrier semaphores. Data moves between devices by JAX's collectives and lax.ppermute only.
A program may use at most 128 MiB of HBM per device.

```python
import math
import jax
import jax.numpy as jnp
from jax import lax

F = 256
TILE = 128
NODES = 65536
TROWS = 32
TCOLS = 32
KMAX = 320
N_ROW = 16
N_COL = 16


def tile_positions(key):
    device_keys = jax.random.split(jax.random.fold_in(key, 11), N_ROW * N_COL)

    def one_device(device_key):
        return jax.random.permutation(device_key, TROWS * TCOLS)[:KMAX]
    chosen = jax.vmap(one_device)(device_keys)
    return chosen.reshape(N_ROW, N_COL, KMAX).astype(jnp.int32)


def draw_tile_rows(key, part):
    return (tile_positions(key) // TCOLS).astype(jnp.int32)


def draw_tile_cols(key, part):
    return (tile_positions(key) % TCOLS).astype(jnp.int32)


def draw_tile_count(key, part):
    first_key = jax.random.fold_in(key, 23)
    second_key = jax.random.fold_in(key, 29)
    ranks = jax.random.randint(first_key, (N_ROW * N_COL,), 0, KMAX)
    counts = KMAX // 8 + ranks * ranks // KMAX * 7 // 8
    fullest = jax.random.randint(second_key, (), 0, N_ROW * N_COL)
    counts = counts.at[fullest].set(KMAX)
    return counts.reshape(N_ROW, N_COL).astype(jnp.int32)


def shard_levels(stream_key, extent, shards, smallest, largest):
    level, own = 1.0, jax.random.fold_in(stream_key, 6)
    for position, shards_of in shards:
        heights = jnp.exp(jax.random.uniform(jax.random.fold_in(own, position), (shards_of,), jnp.float32, smallest / len(shards), largest / len(shards)))
        level = level * jnp.repeat(heights, extent[position] // shards_of).reshape([-1 if axis == position else 1 for axis in range(len(extent))])
    return level


def scatter_about(own_key, extent, deviation, reach, pieces=(), kind=jnp.bfloat16):
    values = deviation * jax.random.normal(own_key, extent, jnp.float32)
    if pieces:
        values = values * shard_levels(own_key, extent, pieces, -0.22, 0.18)
    return jnp.clip(values, -reach, reach).astype(kind)


def setup_inputs(seed: int = 0) -> dict:
    key_list = jax.random.split(jax.random.key(seed), 8)
    features = scatter_about(key_list[0], (NODES, F), 1.0, 6.0, ((0, 256),))
    weight = scatter_about(key_list[1], (F, F), F ** -0.5, 0.375)
    tile_rows = draw_tile_rows(jax.random.fold_in(key_list[7], 71), 0)
    tile_cols = draw_tile_cols(jax.random.fold_in(key_list[7], 71), 0)
    tile_count = draw_tile_count(jax.random.fold_in(key_list[7], 71), 0)
    tile_values = jnp.clip(jnp.exp(math.log(0.049804688) - 3.2155114 * jax.random.uniform(key_list[5], (N_ROW, N_COL, KMAX, TILE, TILE), jnp.float32) ** shard_levels(key_list[5], (N_ROW, N_COL, KMAX, TILE, TILE), ((0, 16), (1, 16)), -0.2, 0.2)), 0.0019989014, 0.049804688).astype(jnp.bfloat16)
    grad_out = scatter_about(key_list[6], (NODES, F), 1.0, 6.0, ((0, 256),))
    return dict(features=features, weight=weight, tile_rows=tile_rows, tile_cols=tile_cols, tile_count=tile_count, tile_values=tile_values, grad_out=grad_out)


def gelu_tanh(value):
    return jax.nn.gelu(value, approximate=True)

def round_half(value):
    rounded = lax.optimization_barrier(value.astype(jnp.bfloat16))
    return rounded.astype(jnp.float32)

def reference(features, weight, tile_rows, tile_cols, tile_count, tile_values, grad_out):
    projected = jnp.dot(features, weight, preferred_element_type=jnp.float32).astype(jnp.bfloat16)
    row_span = NODES // N_ROW
    col_span = NODES // N_COL
    offsets = jnp.arange(TILE, dtype=jnp.int32)
    slot_ids = jnp.arange(KMAX, dtype=jnp.int32)

    def indices(device):
        row_index = (device // N_COL).astype(jnp.int32)
        col_index = (device % N_COL).astype(jnp.int32)
        local_rows = tile_rows[row_index, col_index][:, None] * TILE + offsets[None, :]
        local_cols = tile_cols[row_index, col_index][:, None] * TILE + offsets[None, :]
        live_slots = (slot_ids < tile_count[row_index, col_index]).astype(jnp.float32)
        block_values = tile_values[row_index, col_index].astype(jnp.float32)
        return (row_index, col_index, local_rows, local_cols, live_slots, block_values)

    def forward_one(running_sum, device):
        row_index, col_index, local_rows, local_cols, live_slots, block_values = indices(device)
        picked = projected[col_index * col_span + local_cols].astype(jnp.float32)
        products = jnp.einsum('kab,kbf->kaf', block_values, picked) * live_slots[:, None, None]
        partial_value = jnp.zeros((row_span, F), jnp.float32).at[local_rows.reshape(-1)].add(products.reshape(-1, F))
        partial_value = round_half(partial_value)
        start = (row_index * row_span).astype(jnp.int32)
        current = lax.dynamic_slice_in_dim(running_sum, start, row_span, 0)
        running_sum = lax.dynamic_update_slice_in_dim(running_sum, current + partial_value, start, 0)
        return (running_sum, None)
    devices = jnp.arange(N_ROW * N_COL, dtype=jnp.int32)
    summed, _ = lax.scan(forward_one, jnp.zeros((NODES, F), jnp.float32), devices)
    activations, pullback = jax.vjp(gelu_tanh, summed)
    gradient = pullback(grad_out.astype(jnp.float32))[0].astype(jnp.bfloat16)
    activations = activations.astype(jnp.bfloat16)

    def backward_one(running_sum, device):
        row_index, col_index, local_rows, local_cols, live_slots, block_values = indices(device)
        picked = gradient[row_index * row_span + local_rows].astype(jnp.float32)
        products = jnp.einsum('kab,kaf->kbf', block_values, picked) * live_slots[:, None, None]
        partial_value = jnp.zeros((col_span, F), jnp.float32).at[local_cols.reshape(-1)].add(products.reshape(-1, F))
        partial_value = round_half(partial_value)
        start = (col_index * col_span).astype(jnp.int32)
        current = lax.dynamic_slice_in_dim(running_sum, start, col_span, 0)
        running_sum = lax.dynamic_update_slice_in_dim(running_sum, current + partial_value, start, 0)
        return (running_sum, None)
    back_sum, _ = lax.scan(backward_one, jnp.zeros((NODES, F), jnp.float32), devices)
    back_sum = back_sum.astype(jnp.bfloat16)
    feature_grad = jnp.dot(back_sum, weight.T, preferred_element_type=jnp.float32).astype(jnp.bfloat16)
    weight_grad = jnp.dot(features.T, back_sum, preferred_element_type=jnp.float32) * (1.0 / math.sqrt(NODES))
    return (activations, feature_grad, weight_grad)
```

```python
import functools
import math

import jax
import jax.numpy as jnp
from jax import lax
from jax.experimental import pallas as pl
from jax.experimental.pallas import tpu as pltpu
from jax.sharding import Mesh, PartitionSpec as P


def gelu_tanh(value):
    return jax.nn.gelu(value, approximate=True)


def tile_kernel(count_ref, put_ref, take_ref, tiles_ref, source_ref, out_ref, sum_ref, *, unroll, transpose):
    step = pl.program_id(0)
    group, size, _ = tiles_ref.shape
    spare = sum_ref.shape[0] // size - 1
    live = count_ref[0]
    first = step * group
    contract = (((0,), (0,)), ((), ())) if transpose else (((1,), (0,)), ((), ()))

    @pl.when(step == 0)
    def _():
        sum_ref[...] = jnp.zeros_like(sum_ref)

    def batch(index, carry):
        rows, products = [], []
        for lane in range(unroll):
            place = index * unroll + lane
            slot = first + place
            used = slot < live
            put = jnp.where(used, put_ref[slot], spare)
            take = jnp.where(used, take_ref[slot], 0)
            picked = source_ref[pl.ds(pl.multiple_of(take * size, size), size), :]
            rows.append(pl.multiple_of(put * size, size))
            products.append(
                lax.dot_general(tiles_ref[place], picked, contract, preferred_element_type=jnp.float32)
            )
        for row, product in zip(rows, products):
            sum_ref[pl.ds(row, size), :] += product
        return carry

    todo = jnp.clip(live - first, 0, group)
    lax.fori_loop(0, (todo + unroll - 1) // unroll, batch, 0)

    @pl.when(step == pl.num_programs(0) - 1)
    def _():
        out_ref[...] = sum_ref[pl.ds(0, out_ref.shape[0]), :].astype(out_ref.dtype)


def tile_products(live_count, put_ids, take_ids, block_tiles, source, out_rows, transpose):
    slots, size, _ = block_tiles.shape
    width = source.shape[1]
    group = math.gcd(slots, 32)
    unroll = math.gcd(group, 16)
    return pl.pallas_call(
        functools.partial(tile_kernel, unroll=unroll, transpose=transpose),
        out_shape=jax.ShapeDtypeStruct((out_rows, width), jnp.bfloat16),
        grid_spec=pltpu.PrefetchScalarGridSpec(
            num_scalar_prefetch=3,
            grid=(slots // group,),
            in_specs=[
                pl.BlockSpec(
                    (group, size, size),
                    lambda i, count, put, take: (jnp.minimum(i, jnp.maximum(count[0] - 1, 0) // group), 0, 0),
                ),
                pl.BlockSpec(source.shape, lambda i, *_: (0, 0), pipeline_mode=pl.Buffered(1)),
            ],
            out_specs=pl.BlockSpec((out_rows, width), lambda i, *_: (0, 0)),
            scratch_shapes=[pltpu.VMEM((out_rows + size, width), jnp.float32)],
        ),
        compiler_params=pltpu.CompilerParams(vmem_limit_bytes=40 << 20),
        cost_estimate=pl.CostEstimate(
            flops=2 * slots * size * size * width,
            bytes_accessed=2 * slots * size * size + 4 * out_rows * width,
            transcendentals=0,
        ),
    )(live_count, put_ids, take_ids, block_tiles, source)


def scatter_sum(parts, axes):
    devices = lax.axis_size(axes)
    chunks = parts.reshape(devices, parts.shape[0] // devices, parts.shape[1])
    received = lax.all_to_all(chunks, axes, 0, 0)
    return received.astype(jnp.float32).sum(0)


def on_device(row, col, features, weight, tile_rows, tile_cols, tile_count, tile_values, grad_out):
    seg_rows, feat_width = features.shape
    block_tiles = tile_values[0, 0]
    tile_row_ids = tile_rows[0, 0]
    tile_col_ids = tile_cols[0, 0]
    live_count = tile_count[0]
    row_span = lax.axis_size(col) * seg_rows
    col_span = lax.axis_size(row) * seg_rows
    node_total = seg_rows * lax.axis_size(row) * lax.axis_size(col)

    gathered = features
    for axis in reversed(row):
        gathered = lax.all_gather(gathered, axis, axis=0, tiled=True)
    partial_value = tile_products(
        live_count, tile_row_ids, tile_col_ids, block_tiles, gathered, row_span, False
    )
    aggregated = scatter_sum(partial_value, col).astype(jnp.bfloat16)
    summed = jnp.dot(aggregated, weight, preferred_element_type=jnp.float32)
    activations, pullback = jax.vjp(gelu_tanh, summed)
    gradient = pullback(grad_out.astype(jnp.float32))[0].astype(jnp.bfloat16)
    activations = activations.astype(jnp.bfloat16)
    grad_blocks = lax.all_gather(gradient, col, axis=0, tiled=True)

    local_weight = lax.dot_general(
        aggregated, gradient, (((0,), (0,)), ((), ())), preferred_element_type=jnp.float32
    )
    weight_slice = scatter_sum(local_weight, col)
    weight_slices = lax.all_gather(weight_slice, row, axis=0)
    weight_slice = weight_slices.sum(0) * (1.0 / math.sqrt(node_total))
    weight_grad = lax.all_gather(weight_slice, col, axis=0, tiled=True)

    partial_back = tile_products(
        live_count, tile_col_ids, tile_row_ids, block_tiles, grad_blocks, col_span, True
    )
    back_sum = scatter_sum(partial_back, row).astype(jnp.bfloat16)
    feature_grad = lax.dot_general(
        back_sum, weight, (((1,), (1,)), ((), ())), preferred_element_type=jnp.float32
    ).astype(jnp.bfloat16)
    return (activations, feature_grad, weight_grad)


def solution(mesh):
    row, col = ("row_far", "row_near"), ("col_far", "col_mid", "col_near")
    split = Mesh(mesh.devices.reshape(4, 4, 4, 2, 2), row + col)
    by_row, by_col = P(row + col, None), P(col + row, None)
    placed = (
        by_col,
        P(),
        P(row, col, None),
        P(row, col, None),
        P(row, col),
        P(row, col, None, None, None),
        by_row,
    )
    return jax.shard_map(
        functools.partial(on_device, row, col),
        mesh=split,
        in_specs=placed,
        out_specs=(by_row, by_col, P()),
        check_vma=False,
    )
```

```python
import functools
import math

import jax
import jax.numpy as jnp
from jax import lax
from jax.experimental import pallas as pl
from jax.experimental.pallas import tpu as pltpu
from jax.sharding import Mesh, PartitionSpec as P

def gelu_tanh(value):
    return jax.nn.gelu(value, approximate=True)


def tile_kernel(count_ref, put_ref, take_ref, tiles_ref, *refs, pieces, outs, unroll, transpose):
    piece_refs, out_refs = refs[: len(pieces)], refs[len(pieces) : len(pieces) + outs]
    source_ref, sum_ref, arrived = refs[len(pieces) + outs :]
    step = pl.program_id(0)
    group, size, _ = tiles_ref.shape
    spare = sum_ref.shape[0] // size - 1
    live = count_ref[0]
    first = step * group
    contract = (((0,), (0,)), ((), ())) if transpose else (((1,), (0,)), ((), ()))

    @pl.when(step == 0)
    def _():
        copies, at = [], 0
        for piece, (blocks, rows) in zip(piece_refs, pieces):
            for block in range(blocks):
                copies.append(
                    pltpu.make_async_copy(
                        piece.at[block, pl.ds(0, rows), :],
                        source_ref.at[pl.ds(at, rows), :],
                        arrived.at[len(copies)],
                    )
                )
                at += rows
        for copy in copies:
            copy.start()
        sum_ref[...] = jnp.zeros_like(sum_ref)
        for copy in copies:
            copy.wait()

    def batch(index, carry):
        rows, products = [], []
        for lane in range(unroll):
            place = index * unroll + lane
            slot = first + place
            used = slot < live
            put = jnp.where(used, put_ref[slot], spare)
            take = jnp.where(used, take_ref[slot], 0)
            picked = source_ref[pl.ds(pl.multiple_of(take * size, size), size), :]
            rows.append(pl.multiple_of(put * size, size))
            products.append(
                lax.dot_general(tiles_ref[place], picked, contract, preferred_element_type=jnp.float32)
            )
        for row, product in zip(rows, products):
            sum_ref[pl.ds(row, size), :] += product
        return carry

    todo = jnp.clip(live - first, 0, group)
    lax.fori_loop(0, (todo + unroll - 1) // unroll, batch, 0)

    @pl.when(step == pl.num_programs(0) - 1)
    def _():
        at = 0
        for out in out_refs:
            out[...] = sum_ref[pl.ds(at, out.shape[0]), :].astype(out.dtype)
            at += out.shape[0]


def tile_products(live_count, put_ids, take_ids, block_tiles, sources, rows_used, outs, transpose):
    slots, size, _ = block_tiles.shape
    width = sources[0].shape[-1]
    sources = [source.reshape((-1,) + source.shape[-2:]) for source in sources]
    pieces = [(source.shape[0], rows_used or source.shape[1]) for source in sources]
    source_rows = sum(blocks * rows for blocks, rows in pieces)
    sum_rows = sum(rows for rows, _ in outs)
    group = math.gcd(slots, 32)
    unroll = math.gcd(group, 16)
    whole = lambda i, *_: (0, 0)
    return pl.pallas_call(
        functools.partial(
            tile_kernel, pieces=pieces, outs=len(outs), unroll=unroll, transpose=transpose
        ),
        out_shape=[jax.ShapeDtypeStruct((rows, width), kind) for rows, kind in outs],
        grid_spec=pltpu.PrefetchScalarGridSpec(
            num_scalar_prefetch=3,
            grid=(slots // group,),
            in_specs=[
                pl.BlockSpec(
                    (group, size, size),
                    lambda i, count, put, take: (jnp.minimum(i, jnp.maximum(count[0] - 1, 0) // group), 0, 0),
                )
            ]
            + [pl.BlockSpec(memory_space=pl.ANY)] * len(pieces),
            out_specs=[pl.BlockSpec((rows, width), whole) for rows, _ in outs],
            scratch_shapes=[
                pltpu.VMEM((source_rows, width), jnp.bfloat16),
                pltpu.VMEM((sum_rows + size, width), jnp.float32),
                pltpu.SemaphoreType.DMA((sum(blocks for blocks, _ in pieces),)),
            ],
        ),
        compiler_params=pltpu.CompilerParams(vmem_limit_bytes=56 << 20),
        cost_estimate=pl.CostEstimate(
            flops=8 * slots * size * size * width,
            bytes_accessed=2 * slots * size * size + 4 * sum_rows * width,
            transcendentals=0,
        ),
    )(live_count, put_ids, take_ids, block_tiles, *sources)


def exchange(chunks, axes):
    return lax.all_to_all(chunks, axes, 0, 0)


def spread(block, axes):
    devices = lax.axis_size(axes)
    return exchange(lax.optimization_barrier(jnp.broadcast_to(block[None], (devices,) + block.shape)), axes)


def total(parts):
    return parts.astype(jnp.float32).sum(0)


def shift(block, axis, by):
    devices = lax.axis_size(axis)
    return lax.ppermute(block, axis, [(k, (k + by) % devices) for k in range(devices)])


def on_device(features, weight, tile_rows, tile_cols, tile_count, tile_values, grad_out):
    seg_rows, feat_width = features.shape
    block_tiles = tile_values[0, 0]
    size = block_tiles.shape[-1]
    live_count = tile_count[0]
    tile_row_ids = tile_rows[0, 0]
    tile_col_ids = tile_cols[0, 0]
    far, near = lax.axis_size("row_far"), lax.axis_size("row_near")
    mid = lax.axis_size(("col_far", "col_mid"))
    row, col = ("row_far", "row_near"), ("col_far", "col_mid", "col_near")
    node_total = seg_rows * lax.axis_size(row) * lax.axis_size(col)
    seg_tiles = seg_rows // size
    far_rows, mid_rows = near * seg_rows, mid * seg_rows
    far_tiles = near * seg_tiles
    half_tiles, half_rows = far_tiles // 2, far_rows // 2

    away = (tile_col_ids // far_tiles - lax.axis_index("row_far")) % far
    inner = tile_col_ids % far_tiles
    upper = inner >= half_tiles
    col_take = jnp.where(away == 0, 0, jnp.where(away == 3, 1, away + 1)) * far_tiles + inner
    col_put = (
        jnp.where(
            away == 0,
            0,
            jnp.where(
                away == 1,
                jnp.where(upper, 1 * far_tiles, 3 * far_tiles),
                jnp.where(
                    away == 2,
                    jnp.where(upper, 2 * far_tiles, 1 * far_tiles),
                    jnp.where(upper, 3 * far_tiles, 2 * far_tiles),
                ),
            ),
        )
        + inner
    )
    other = (tile_row_ids // seg_tiles) % 2 != lax.axis_index("col_near")
    row_place = (
        other.astype(jnp.int32) * (mid * seg_tiles)
        + tile_row_ids // (2 * seg_tiles) * seg_tiles
        + tile_row_ids % seg_tiles
    )

    own = lax.all_gather(features, "row_near", axis=0, tiled=True)
    left, right = shift(own, "row_far", 1), shift(own, "row_far", -1)
    low, high = shift(left[:half_rows], "row_far", 1), shift(right[half_rows:], "row_far", -1)
    keep, send = tile_products(
        live_count, row_place, col_take, block_tiles, [own, left, right, low, high], None,
        [(mid_rows, jnp.float32), (mid_rows, jnp.bfloat16)], False,
    )
    paired = (keep + shift(send, "col_near", 1).astype(jnp.float32)).astype(jnp.bfloat16)
    parts = exchange(paired.reshape(mid, seg_rows, feat_width), ("col_far", "col_mid"))
    aggregated = total(parts).astype(jnp.bfloat16)

    summed = jnp.dot(aggregated, weight, preferred_element_type=jnp.float32)
    activations, pullback = jax.vjp(gelu_tanh, summed)
    gradient = pullback(grad_out.astype(jnp.float32))[0].astype(jnp.bfloat16)
    activations = activations.astype(jnp.bfloat16)

    local_weight = lax.dot_general(
        aggregated, gradient, (((0,), (0,)), ((), ())), preferred_element_type=jnp.float32
    ).astype(jnp.bfloat16)
    load = jnp.concatenate(
        [
            jnp.broadcast_to(gradient[None], (mid,) + gradient.shape),
            local_weight.reshape(mid, -1, feat_width),
        ],
        axis=1,
    )
    mine = exchange(load, ("col_far", "col_mid"))
    theirs = shift(mine, "col_near", 1)
    weight_pair = total(mine[:, seg_rows:]) + total(theirs[:, seg_rows:])
    weight_rows = feat_width // lax.axis_size(col)
    weight_slice = lax.dynamic_slice_in_dim(weight_pair, lax.axis_index("col_near") * weight_rows, weight_rows, 0)
    weight_slices = jnp.broadcast_to(weight_slice[None], (lax.axis_size(row),) + weight_slice.shape)
    mine, theirs, weight_slices = lax.optimization_barrier((mine, theirs, weight_slices))
    weight_slices = exchange(weight_slices, row)

    own, right_one, left_one, right_two, left_two = tile_products(
        live_count, col_put, row_place, block_tiles, [mine, theirs], seg_rows,
        [
            (far_rows, jnp.float32),
            (far_rows, jnp.bfloat16),
            (far_rows, jnp.bfloat16),
            (half_rows, jnp.float32),
            (half_rows, jnp.float32),
        ],
        True,
    )
    right_one, left_one, weight_slices = lax.optimization_barrier((right_one, left_one, weight_slices))
    from_left, from_right = shift(right_one, "row_far", 1), shift(left_one, "row_far", -1)
    weight_slice = total(weight_slices) * (1.0 / math.sqrt(node_total))
    weight_grad = spread(weight_slice, col).reshape(feat_width, feat_width)
    from_left, from_right, weight_grad = lax.optimization_barrier((from_left, from_right, weight_grad))
    right_two = (right_two + from_left[:half_rows].astype(jnp.float32)).astype(jnp.bfloat16)
    left_two = (left_two + from_right[half_rows:].astype(jnp.float32)).astype(jnp.bfloat16)
    low, high = shift(right_two, "row_far", 1), shift(left_two, "row_far", -1)
    low = own[:half_rows] + low.astype(jnp.float32) + from_right[:half_rows].astype(jnp.float32)
    high = own[half_rows:] + high.astype(jnp.float32) + from_left[half_rows:].astype(jnp.float32)
    mixed = jnp.concatenate([low, high], axis=0).astype(jnp.bfloat16)
    parts = exchange(mixed.reshape(near, seg_rows, feat_width), "row_near")
    back_sum = total(parts).astype(jnp.bfloat16)

    feature_grad = lax.dot_general(
        back_sum, weight, (((1,), (1,)), ((), ())), preferred_element_type=jnp.float32
    ).astype(jnp.bfloat16)
    return (activations, feature_grad, weight_grad)


def solution(mesh):
    row, col = ("row_far", "row_near"), ("col_far", "col_mid", "col_near")
    split = Mesh(mesh.devices.reshape(4, 4, 4, 2, 2), row + col)
    by_row, by_col = P(row + col, None), P(col + row, None)
    placed = (
        by_col,
        P(),
        P(row, col, None),
        P(row, col, None),
        P(row, col),
        P(row, col, None, None, None),
        by_row,
    )
    return jax.shard_map(
        on_device,
        mesh=split,
        in_specs=placed,
        out_specs=(by_row, by_col, P()),
        check_vma=False,
    )
```

```python
import functools
import math

import jax
import jax.numpy as jnp
from jax import lax
from jax.experimental import pallas as pl
from jax.experimental.pallas import tpu as pltpu
from jax.sharding import Mesh, PartitionSpec as P

def gelu_tanh(value):
    return jax.nn.gelu(value, approximate=True)


def tile_kernel(count_ref, put_ref, take_ref, tiles_hbm, *refs, pieces, outs, group, transpose):
    piece_refs, out_refs = refs[: len(pieces)], refs[len(pieces) : len(pieces) + len(outs)]
    tiles_ref, source_ref, sum_ref, *rounded, tiles_in, source_in, out_sent = refs[len(pieces) + len(outs) :]
    size = tiles_ref.shape[-1]
    spare = sum_ref.shape[0] // size - 1
    live = count_ref[0]
    contract = (((0,), (0,)), ((), ())) if transpose else (((1,), (0,)), ((), ()))

    def tiles_copy(index):
        some = pl.ds(pl.multiple_of(index * group, group), group)
        return pltpu.make_async_copy(tiles_hbm.at[some], tiles_ref.at[some], tiles_in.at[index])

    copies, at = [], 0
    for piece, (blocks, rows) in zip(piece_refs, pieces):
        for block in range(blocks):
            copies.append(
                pltpu.make_async_copy(
                    piece.at[block, pl.ds(0, rows), :],
                    source_ref.at[pl.ds(at, rows), :],
                    source_in.at[len(copies)],
                )
            )
            at += rows
    for copy in copies:
        copy.start()
    batches = (live + group - 1) // group

    def begin(index, carry):
        tiles_copy(index).start()
        return carry

    lax.fori_loop(0, batches, begin, 0)
    sum_ref[...] = jnp.zeros_like(sum_ref)
    for copy in copies:
        copy.wait()

    def batch(index, carry):
        tiles_copy(index).wait()
        rows, products = [], []
        for lane in range(group):
            slot = index * group + lane
            used = slot < live
            put = jnp.where(used, put_ref[slot], spare)
            take = jnp.where(used, take_ref[slot], 0)
            picked = source_ref[pl.ds(pl.multiple_of(take * size, size), size), :]
            rows.append(pl.multiple_of(put * size, size))
            products.append(
                lax.dot_general(tiles_ref[slot], picked, contract, preferred_element_type=jnp.float32)
            )
        for row, product in zip(rows, products):
            sum_ref[pl.ds(row, size), :] += product
        return carry

    lax.fori_loop(0, batches, batch, 0)

    writes, at = [], 0
    for out in out_refs:
        part = sum_ref.at[pl.ds(at, out.shape[0]), :]
        at += out.shape[0]
        if out.dtype != sum_ref.dtype:
            narrow = rounded.pop(0)
            narrow[...] = part[...].astype(out.dtype)
            part = narrow
        writes.append(pltpu.make_async_copy(part, out, out_sent.at[len(writes)]))
        writes[-1].start()
    for write in writes:
        write.wait()


def tile_products(live_count, put_ids, take_ids, block_tiles, sources, rows_used, outs, transpose):
    slots, size, _ = block_tiles.shape
    width = sources[0].shape[-1]
    sources = [source.reshape((-1,) + source.shape[-2:]) for source in sources]
    pieces = [(source.shape[0], rows_used or source.shape[1]) for source in sources]
    source_rows = sum(blocks * rows for blocks, rows in pieces)
    sum_rows = sum(rows for rows, _ in outs)
    group = math.gcd(slots, 32)
    anywhere = pl.BlockSpec(memory_space=pl.ANY)
    return pl.pallas_call(
        functools.partial(tile_kernel, pieces=pieces, outs=outs, group=group, transpose=transpose),
        out_shape=[jax.ShapeDtypeStruct((rows, width), kind) for rows, kind in outs],
        in_specs=[pl.BlockSpec(memory_space=pltpu.SMEM)] * 3 + [anywhere] * (1 + len(sources)),
        out_specs=[anywhere] * len(outs),
        scratch_shapes=[
            pltpu.VMEM((slots, size, size), jnp.bfloat16),
            pltpu.VMEM((source_rows, width), jnp.bfloat16),
            pltpu.VMEM((sum_rows + size, width), jnp.float32),
        ]
        + [pltpu.VMEM((rows, width), kind) for rows, kind in outs if kind != jnp.float32]
        + [
            pltpu.SemaphoreType.DMA((slots // group,)),
            pltpu.SemaphoreType.DMA((sum(blocks for blocks, _ in pieces),)),
            pltpu.SemaphoreType.DMA((len(outs),)),
        ],
        compiler_params=pltpu.CompilerParams(vmem_limit_bytes=56 << 20),
        cost_estimate=pl.CostEstimate(
            flops=8 * slots * size * size * width,
            bytes_accessed=2 * slots * size * size + 4 * sum_rows * width,
            transcendentals=0,
        ),
    )(live_count, put_ids, take_ids, block_tiles, *sources)


def exchange(chunks, axes):
    return lax.all_to_all(chunks, axes, 0, 0)


def spread(block, axes):
    devices = lax.axis_size(axes)
    return exchange(lax.optimization_barrier(jnp.broadcast_to(block[None], (devices,) + block.shape)), axes)


def add(*parts):
    return sum(part.astype(jnp.float32) for part in parts).astype(jnp.bfloat16)


def total(parts):
    return parts.astype(jnp.float32).sum(0)


def shift(block, axis, by):
    devices = lax.axis_size(axis)
    return lax.ppermute(block, axis, [(k, (k + by) % devices) for k in range(devices)])


def on_device(features, weight, tile_rows, tile_cols, tile_count, tile_values, grad_out):
    seg_rows, feat_width = features.shape
    block_tiles = tile_values[0, 0]
    size = block_tiles.shape[-1]
    live_count = tile_count[0]
    tile_row_ids = tile_rows[0, 0]
    tile_col_ids = tile_cols[0, 0]
    far, near = lax.axis_size("row_far"), lax.axis_size("row_near")
    mid = lax.axis_size(("col_far", "col_mid"))
    row, col = ("row_far", "row_near"), ("col_far", "col_mid", "col_near")
    node_total = seg_rows * lax.axis_size(row) * lax.axis_size(col)
    seg_tiles = seg_rows // size
    far_rows, mid_rows = near * seg_rows, mid * seg_rows
    far_tiles = near * seg_tiles
    half_tiles, half_rows = far_tiles // 2, far_rows // 2

    away = (tile_col_ids // far_tiles - lax.axis_index("row_far")) % far
    inner = tile_col_ids % far_tiles
    upper = inner >= half_tiles
    col_take = jnp.where(away == 0, 0, jnp.where(away == 3, 1, away + 1)) * far_tiles + inner
    col_put = (
        jnp.where(
            away == 0,
            0,
            jnp.where(
                away == 1,
                jnp.where(upper, 1 * far_tiles, 3 * far_tiles),
                jnp.where(
                    away == 2,
                    jnp.where(upper, 2 * far_tiles, 1 * far_tiles),
                    jnp.where(upper, 3 * far_tiles, 2 * far_tiles),
                ),
            ),
        )
        + inner
    )
    other = (tile_row_ids // seg_tiles) % 2 != lax.axis_index("col_near")
    row_place = (
        other.astype(jnp.int32) * (mid * seg_tiles)
        + tile_row_ids // (2 * seg_tiles) * seg_tiles
        + tile_row_ids % seg_tiles
    )

    own = lax.all_gather(features, "row_near", axis=0, tiled=True)
    left, right = shift(own, "row_far", 1), shift(own, "row_far", -1)
    low, high = shift(left[:half_rows], "row_far", 1), shift(right[half_rows:], "row_far", -1)
    keep, send = tile_products(
        live_count, row_place, col_take, block_tiles, [own, left, right, low, high], None,
        [(mid_rows, jnp.bfloat16)] * 2, False,
    )
    paired = add(keep, shift(send, "col_near", 1))
    parts = exchange(paired.reshape(mid, seg_rows, feat_width), ("col_far", "col_mid"))
    aggregated = total(parts).astype(jnp.bfloat16)

    summed = jnp.dot(aggregated, weight, preferred_element_type=jnp.float32)
    activations, pullback = jax.vjp(gelu_tanh, summed)
    gradient = pullback(grad_out.astype(jnp.float32))[0].astype(jnp.bfloat16)
    activations = activations.astype(jnp.bfloat16)

    local_weight = lax.dot_general(
        aggregated, gradient, (((0,), (0,)), ((), ())), preferred_element_type=jnp.float32
    ).astype(jnp.bfloat16)
    load = jnp.concatenate(
        [
            jnp.broadcast_to(gradient[None], (mid,) + gradient.shape),
            local_weight.reshape(mid, -1, feat_width),
        ],
        axis=1,
    )
    mine = exchange(load, ("col_far", "col_mid"))
    theirs = shift(mine, "col_near", 1)
    weight_pair = total(mine[:, seg_rows:]) + total(theirs[:, seg_rows:])
    weight_rows = feat_width // lax.axis_size(col)
    weight_slice = lax.dynamic_slice_in_dim(weight_pair, lax.axis_index("col_near") * weight_rows, weight_rows, 0)
    weight_slices = jnp.broadcast_to(weight_slice[None], (lax.axis_size(row),) + weight_slice.shape)
    mine, theirs, weight_slices = lax.optimization_barrier((mine, theirs, weight_slices))
    weight_slices = exchange(weight_slices, row)

    own, right_one, left_one, right_two, left_two = tile_products(
        live_count, col_put, row_place, block_tiles, [mine, theirs], seg_rows,
        [(far_rows, jnp.bfloat16)] * 3 + [(half_rows, jnp.bfloat16)] * 2,
        True,
    )
    right_one, left_one, weight_slices = lax.optimization_barrier((right_one, left_one, weight_slices))
    from_left, from_right = shift(right_one, "row_far", 1), shift(left_one, "row_far", -1)
    weight_slice = total(weight_slices) * (1.0 / math.sqrt(node_total))
    weight_grad = spread(weight_slice, col).reshape(feat_width, feat_width)
    from_left, from_right, weight_grad = lax.optimization_barrier((from_left, from_right, weight_grad))
    right_two, left_two = add(right_two, from_left[:half_rows]), add(left_two, from_right[half_rows:])
    low, high = shift(right_two, "row_far", 1), shift(left_two, "row_far", -1)
    low = add(own[:half_rows], low, from_right[:half_rows])
    high = add(own[half_rows:], high, from_left[half_rows:])
    mixed = jnp.concatenate([low, high], axis=0)
    parts = exchange(mixed.reshape(near, seg_rows, feat_width), "row_near")
    back_sum = total(parts).astype(jnp.bfloat16)

    feature_grad = lax.dot_general(
        back_sum, weight, (((1,), (1,)), ((), ())), preferred_element_type=jnp.float32
    ).astype(jnp.bfloat16)
    return (activations, feature_grad, weight_grad)


def solution(mesh):
    row, col = ("row_far", "row_near"), ("col_far", "col_mid", "col_near")
    split = Mesh(mesh.devices.reshape(4, 4, 4, 2, 2), row + col)
    by_row, by_col = P(row + col, None), P(col + row, None)
    placed = (
        by_col,
        P(),
        P(row, col, None),
        P(row, col, None),
        P(row, col),
        P(row, col, None, None, None),
        by_row,
    )
    return jax.shard_map(
        on_device,
        mesh=split,
        in_specs=placed,
        out_specs=(by_row, by_col, P()),
        check_vma=False,
    )
```

```python
import functools
import math

import jax
import jax.numpy as jnp
from jax import lax
from jax.experimental import pallas as pl
from jax.experimental.pallas import tpu as pltpu
from jax.sharding import Mesh, PartitionSpec as P

def gelu_tanh(value):
    return jax.nn.gelu(value, approximate=True)


def tile_kernel(count_ref, put_ref, slot_ref, take_ref, tiles_hbm, *refs, pieces, outs, group, transpose):
    piece_refs, out_refs = refs[: len(pieces)], refs[len(pieces) : len(pieces) + outs]
    tiles_ref, source_ref, sum_ref, *rounded, tiles_in, source_in, out_sent = refs[len(pieces) + outs :]
    size = tiles_ref.shape[-1]
    batches = (count_ref[0] + group - 1) // group

    def fetch(index):
        for lane in range(2 * group):
            place = index * 2 * group + lane
            pltpu.make_async_copy(tiles_hbm.at[slot_ref[place]], tiles_ref.at[place], tiles_in.at[index]).start()

    def fetched(index):
        some = pl.ds(pl.multiple_of(index * 2 * group, 2 * group), 2 * group)
        pltpu.make_async_copy(tiles_hbm.at[pl.ds(0, 2 * group)], tiles_ref.at[some], tiles_in.at[index]).wait()

    contract = (((0,), (0,)), ((), ())) if transpose else (((1,), (0,)), ((), ()))

    copies, at = [], 0
    for piece, (blocks, rows) in zip(piece_refs, pieces):
        for block in range(blocks):
            copies.append(
                pltpu.make_async_copy(
                    piece.at[block, pl.ds(0, rows), :],
                    source_ref.at[pl.ds(at, rows), :],
                    source_in.at[len(copies)],
                )
            )
            at += rows
    for copy in copies:
        copy.start()
    fetch(0)
    for index in range(1, AHEAD):
        pl.when(index < batches)(functools.partial(fetch, index))
    source_ref[pl.ds(at, size), :] = jnp.zeros((size, source_ref.shape[1]), source_ref.dtype)
    sum_ref[...] = jnp.zeros_like(sum_ref)
    for copy in copies:
        copy.wait()

    def batch(index, carry):
        pl.when(index + AHEAD < batches)(lambda: fetch(index + AHEAD))
        fetched(index)
        rows, products = [], []
        for lane in range(group):
            pair = index * group + lane
            tiles, picked = [], []
            for place in (2 * pair, 2 * pair + 1):
                take = pl.multiple_of(take_ref[place] * size, size)
                tiles.append(tiles_ref[place])
                picked.append(source_ref[pl.ds(take, size), :])
            rows.append(pl.multiple_of(put_ref[pair] * size, size))
            products.append(
                lax.dot_general(
                    jnp.concatenate(tiles, axis=0 if transpose else 1),
                    jnp.concatenate(picked, axis=0),
                    contract,
                    preferred_element_type=jnp.float32,
                )
            )
        for row, product in zip(rows, products):
            sum_ref[pl.ds(row, size), :] += product
        return carry

    lax.fori_loop(0, batches, batch, 0)

    writes, at = [], 0
    for out, narrow in zip(out_refs, rounded):
        narrow[...] = sum_ref[pl.ds(at, out.shape[0]), :].astype(out.dtype)
        writes.append(pltpu.make_async_copy(narrow, out, out_sent.at[len(writes)]))
        writes[-1].start()
        at += out.shape[0]
    for write in writes:
        write.wait()


PAIRS_AT_ONCE = 16
AHEAD = 4


def pair_up(live_count, put_ids, take_ids, put_blocks, take_blocks):
    slots = put_ids.shape[0]
    slot = jnp.arange(slots, dtype=jnp.int32)
    block = jnp.arange(put_blocks, dtype=jnp.int32)
    put_ids = jnp.where(slot < live_count, put_ids, put_blocks)
    rank = ((put_ids[:, None] == put_ids[None, :]) & (slot[None, :] < slot[:, None])).astype(jnp.int32).sum(1)
    pairs_of = ((put_ids[:, None] == block[None, :]).astype(jnp.int32).sum(0) + 1) // 2
    first = 2 * jnp.where(block[None, :] < put_ids[:, None], pairs_of[None, :], 0).sum(1)
    place = jnp.where(put_ids < put_blocks, first + rank, -1)
    pair_count = pairs_of.sum()
    room = -(-(slots + put_blocks) // (2 * PAIRS_AT_ONCE)) * PAIRS_AT_ONCE
    pair = jnp.arange(room, dtype=jnp.int32)
    spot = jnp.arange(2 * room, dtype=jnp.int32)
    here = place[None, :] == spot[:, None]
    slot_ids = jnp.where(here, slot[None, :], 0).sum(1)
    take_ids = jnp.where(here, take_ids[None, :] - take_blocks, 0).sum(1) + take_blocks
    pair_put = jnp.where(place[None, :] == 2 * pair[:, None], put_ids[None, :] - put_blocks, 0).sum(1) + put_blocks
    return pair_count.reshape(1), pair_put, slot_ids, take_ids


def tile_products(pairs, block_tiles, sources, rows_used, outs, transpose):
    slots, size, _ = block_tiles.shape
    width = sources[0].shape[-1]
    sources = [source.reshape((-1,) + source.shape[-2:]) for source in sources]
    pieces = [(source.shape[0], rows_used or source.shape[1]) for source in sources]
    source_rows = sum(blocks * rows for blocks, rows in pieces)
    sum_rows = sum(outs)
    places = pairs[2].shape[0]
    anywhere = pl.BlockSpec(memory_space=pl.ANY)
    return pl.pallas_call(
        functools.partial(tile_kernel, pieces=pieces, outs=len(outs), group=PAIRS_AT_ONCE, transpose=transpose),
        out_shape=[jax.ShapeDtypeStruct((rows, width), jnp.bfloat16) for rows in outs],
        in_specs=[pl.BlockSpec(memory_space=pltpu.SMEM)] * 4
        + [anywhere] * (1 + len(sources)),
        out_specs=[anywhere] * len(outs),
        scratch_shapes=[
            pltpu.VMEM((places, size, size), jnp.bfloat16),
            pltpu.VMEM((source_rows + size, width), jnp.bfloat16),
            pltpu.VMEM((sum_rows + size, width), jnp.float32),
        ]
        + [pltpu.VMEM((rows, width), jnp.bfloat16) for rows in outs]
        + [
            pltpu.SemaphoreType.DMA((places // (2 * PAIRS_AT_ONCE),)),
            pltpu.SemaphoreType.DMA((sum(blocks for blocks, _ in pieces),)),
            pltpu.SemaphoreType.DMA((len(outs),)),
        ],
        compiler_params=pltpu.CompilerParams(vmem_limit_bytes=(56 if transpose else 48) << 20),
        cost_estimate=pl.CostEstimate(
            flops=8 * slots * size * size * width,
            bytes_accessed=2 * slots * size * size + 4 * sum_rows * width,
            transcendentals=0,
        ),
    )(*pairs, block_tiles, *sources)


def exchange(chunks, axes):
    return lax.all_to_all(chunks, axes, 0, 0)


def spread(block, axes):
    devices = lax.axis_size(axes)
    return exchange(lax.optimization_barrier(jnp.broadcast_to(block[None], (devices,) + block.shape)), axes)


def add(*parts):
    return sum(part.astype(jnp.float32) for part in parts).astype(jnp.bfloat16)


def total(parts):
    return parts.astype(jnp.float32).sum(0)


def shift(block, axis, by):
    devices = lax.axis_size(axis)
    return lax.ppermute(block, axis, [(k, (k + by) % devices) for k in range(devices)])


def on_device(features, weight, tile_rows, tile_cols, tile_count, tile_values, grad_out):
    seg_rows, feat_width = features.shape
    block_tiles = tile_values[0, 0]
    size = block_tiles.shape[-1]
    live_count = tile_count[0, 0]
    tile_row_ids = tile_rows[0, 0]
    tile_col_ids = tile_cols[0, 0]
    far, near = lax.axis_size("row_far"), lax.axis_size("row_near")
    mid = lax.axis_size(("col_far", "col_mid"))
    row, col = ("row_far", "row_near"), ("col_far", "col_mid", "col_near")
    node_total = seg_rows * lax.axis_size(row) * lax.axis_size(col)
    seg_tiles = seg_rows // size
    far_rows, mid_rows = near * seg_rows, mid * seg_rows
    far_tiles = near * seg_tiles
    half_tiles, half_rows = far_tiles // 2, far_rows // 2

    away = (tile_col_ids // far_tiles - lax.axis_index("row_far")) % far
    inner = tile_col_ids % far_tiles
    upper = inner >= half_tiles
    col_take = jnp.where(away == 0, 0, jnp.where(away == 3, 1, away + 1)) * far_tiles + inner
    col_put = (
        jnp.where(
            away == 0,
            0,
            jnp.where(
                away == 1,
                jnp.where(upper, 1 * far_tiles, 3 * far_tiles),
                jnp.where(
                    away == 2,
                    jnp.where(upper, 2 * far_tiles, 1 * far_tiles),
                    jnp.where(upper, 3 * far_tiles, 2 * far_tiles),
                ),
            ),
        )
        + inner
    )
    other = (tile_row_ids // seg_tiles) % 2 != lax.axis_index("col_near")
    row_place = (
        other.astype(jnp.int32) * (mid * seg_tiles)
        + tile_row_ids // (2 * seg_tiles) * seg_tiles
        + tile_row_ids % seg_tiles
    )

    row_tiles, col_tiles = lax.axis_size(col) * seg_tiles, lax.axis_size(row) * seg_tiles
    row_pairs = pair_up(live_count, row_place, col_take, row_tiles, col_tiles)
    col_pairs = pair_up(live_count, col_put, row_place, col_tiles, row_tiles)

    own = lax.all_gather(features, "row_near", axis=0, tiled=True)
    left, right = shift(own, "row_far", 1), shift(own, "row_far", -1)
    low, high = shift(left[:half_rows], "row_far", 1), shift(right[half_rows:], "row_far", -1)
    keep, send = tile_products(
        row_pairs, block_tiles, [own, left, right, low, high], None, [mid_rows] * 2, False
    )
    paired = add(keep, shift(send, "col_near", 1))
    parts = exchange(paired.reshape(mid, seg_rows, feat_width), ("col_far", "col_mid"))
    aggregated = total(parts).astype(jnp.bfloat16)

    summed = jnp.dot(aggregated, weight, preferred_element_type=jnp.float32)
    activations, pullback = jax.vjp(gelu_tanh, summed)
    gradient = pullback(grad_out.astype(jnp.float32))[0].astype(jnp.bfloat16)
    activations = activations.astype(jnp.bfloat16)

    local_weight = lax.dot_general(
        aggregated, gradient, (((0,), (0,)), ((), ())), preferred_element_type=jnp.float32
    ).astype(jnp.bfloat16)
    load = jnp.concatenate(
        [
            jnp.broadcast_to(gradient[None], (mid,) + gradient.shape),
            local_weight.reshape(mid, -1, feat_width),
        ],
        axis=1,
    )
    mine = exchange(load, ("col_far", "col_mid"))
    theirs = shift(mine, "col_near", 1)
    weight_pair = total(mine[:, seg_rows:]) + total(theirs[:, seg_rows:])
    weight_rows = feat_width // lax.axis_size(col)
    weight_slice = lax.dynamic_slice_in_dim(weight_pair, lax.axis_index("col_near") * weight_rows, weight_rows, 0)
    weight_slices = jnp.broadcast_to(weight_slice[None], (lax.axis_size(row),) + weight_slice.shape)
    mine, theirs, weight_slices = lax.optimization_barrier((mine, theirs, weight_slices))
    weight_slices = exchange(weight_slices, row)

    own, right_one, left_one, right_two, left_two = tile_products(
        col_pairs, block_tiles, [mine, theirs], seg_rows, [far_rows] * 3 + [half_rows] * 2, True
    )
    right_one, left_one, weight_slices = lax.optimization_barrier((right_one, left_one, weight_slices))
    from_left, from_right = shift(right_one, "row_far", 1), shift(left_one, "row_far", -1)
    weight_slice = total(weight_slices) * (1.0 / math.sqrt(node_total))
    weight_grad = spread(weight_slice, col).reshape(feat_width, feat_width)
    from_left, from_right, weight_grad = lax.optimization_barrier((from_left, from_right, weight_grad))
    right_two, left_two = add(right_two, from_left[:half_rows]), add(left_two, from_right[half_rows:])
    low, high = shift(right_two, "row_far", 1), shift(left_two, "row_far", -1)
    low = add(own[:half_rows], low, from_right[:half_rows])
    high = add(own[half_rows:], high, from_left[half_rows:])
    mixed = jnp.concatenate([low, high], axis=0)
    parts = exchange(mixed.reshape(near, seg_rows, feat_width), "row_near")
    back_sum = total(parts).astype(jnp.bfloat16)

    feature_grad = lax.dot_general(
        back_sum, weight, (((1,), (1,)), ((), ())), preferred_element_type=jnp.float32
    ).astype(jnp.bfloat16)
    return (activations, feature_grad, weight_grad)


def solution(mesh):
    row, col = ("row_far", "row_near"), ("col_far", "col_mid", "col_near")
    split = Mesh(mesh.devices.reshape(4, 4, 4, 2, 2), row + col)
    by_row, by_col = P(row + col, None), P(col + row, None)
    placed = (
        by_col,
        P(),
        P(row, col, None),
        P(row, col, None),
        P(row, col),
        P(row, col, None, None, None),
        by_row,
    )
    return jax.shard_map(
        on_device,
        mesh=split,
        in_specs=placed,
        out_specs=(by_row, by_col, P()),
        check_vma=False,
    )
```

```python
import functools
import math

import jax
import jax.numpy as jnp
from jax import lax
from jax.experimental import pallas as pl
from jax.experimental.pallas import tpu as pltpu
from jax.sharding import Mesh, PartitionSpec as P

def gelu_tanh(value):
    return jax.nn.gelu(value, approximate=True)


def tile_kernel(count_ref, put_ref, slot_ref, take_ref, tiles_hbm, *refs, pieces, outs, group, transpose):
    piece_refs, out_refs = refs[: len(pieces)], refs[len(pieces) : len(pieces) + outs]
    tiles_ref, source_ref, sum_ref, *rounded, tiles_in, source_in, out_sent = refs[len(pieces) + outs :]
    size = tiles_ref.shape[-1]
    batches = (count_ref[0] + group - 1) // group

    def fetch(index):
        for lane in range(2 * group):
            place = index * 2 * group + lane
            pltpu.make_async_copy(tiles_hbm.at[slot_ref[place]], tiles_ref.at[place], tiles_in.at[index]).start()

    def fetched(index):
        some = pl.ds(pl.multiple_of(index * 2 * group, 2 * group), 2 * group)
        pltpu.make_async_copy(tiles_hbm.at[pl.ds(0, 2 * group)], tiles_ref.at[some], tiles_in.at[index]).wait()

    contract = (((0,), (0,)), ((), ())) if transpose else (((1,), (0,)), ((), ()))

    copies, at = [], 0
    for piece, (blocks, rows) in zip(piece_refs, pieces):
        for block in range(blocks):
            copies.append(
                pltpu.make_async_copy(
                    piece.at[block, pl.ds(0, rows), :],
                    source_ref.at[pl.ds(at, rows), :],
                    source_in.at[len(copies)],
                )
            )
            at += rows
    for copy in copies:
        copy.start()
    fetch(0)
    for index in range(1, AHEAD):
        pl.when(index < batches)(functools.partial(fetch, index))
    source_ref[pl.ds(at, size), :] = jnp.zeros((size, source_ref.shape[1]), source_ref.dtype)
    sum_ref[...] = jnp.zeros_like(sum_ref)
    for copy in copies:
        copy.wait()

    def batch(index, carry):
        pl.when(index + AHEAD < batches)(lambda: fetch(index + AHEAD))
        fetched(index)
        rows, products = [], []
        for lane in range(group):
            pair = index * group + lane
            tiles, picked = [], []
            for place in (2 * pair, 2 * pair + 1):
                take = pl.multiple_of(take_ref[place] * size, size)
                tiles.append(tiles_ref[place])
                picked.append(source_ref[pl.ds(take, size), :])
            rows.append(pl.multiple_of(put_ref[pair] * size, size))
            products.append(
                lax.dot_general(
                    jnp.concatenate(tiles, axis=0 if transpose else 1),
                    jnp.concatenate(picked, axis=0),
                    contract,
                    preferred_element_type=jnp.float32,
                )
            )
        for row, product in zip(rows, products):
            sum_ref[pl.ds(row, size), :] += product
        return carry

    lax.fori_loop(0, batches, batch, 0)

    writes, at = [], 0
    for out, narrow in zip(out_refs, rounded):
        narrow[...] = sum_ref[pl.ds(at, out.shape[0]), :].astype(out.dtype)
        writes.append(pltpu.make_async_copy(narrow, out, out_sent.at[len(writes)]))
        writes[-1].start()
        at += out.shape[0]
    for write in writes:
        write.wait()


PAIRS_AT_ONCE = 16
AHEAD = 4


def pair_up(live_count, put_ids, take_ids, put_blocks, take_blocks):
    slots = put_ids.shape[0]
    slot = jnp.arange(slots, dtype=jnp.int32)
    block = jnp.arange(put_blocks, dtype=jnp.int32)
    put_ids = jnp.where(slot < live_count, put_ids, put_blocks)
    rank = ((put_ids[:, None] == put_ids[None, :]) & (slot[None, :] < slot[:, None])).astype(jnp.int32).sum(1)
    pairs_of = ((put_ids[:, None] == block[None, :]).astype(jnp.int32).sum(0) + 1) // 2
    first = 2 * jnp.where(block[None, :] < put_ids[:, None], pairs_of[None, :], 0).sum(1)
    place = jnp.where(put_ids < put_blocks, first + rank, -1)
    pair_count = pairs_of.sum()
    room = -(-(slots + put_blocks) // (2 * PAIRS_AT_ONCE)) * PAIRS_AT_ONCE
    pair = jnp.arange(room, dtype=jnp.int32)
    spot = jnp.arange(2 * room, dtype=jnp.int32)
    here = place[None, :] == spot[:, None]
    slot_ids = jnp.where(here, slot[None, :], 0).sum(1)
    take_ids = jnp.where(here, take_ids[None, :] - take_blocks, 0).sum(1) + take_blocks
    pair_put = jnp.where(place[None, :] == 2 * pair[:, None], put_ids[None, :] - put_blocks, 0).sum(1) + put_blocks
    return pair_count.reshape(1), pair_put, slot_ids, take_ids


def tile_products(pairs, block_tiles, sources, rows_used, outs, transpose):
    slots, size, _ = block_tiles.shape
    width = sources[0].shape[-1]
    sources = [source.reshape((-1,) + source.shape[-2:]) for source in sources]
    pieces = [(source.shape[0], rows_used or source.shape[1]) for source in sources]
    source_rows = sum(blocks * rows for blocks, rows in pieces)
    sum_rows = sum(outs)
    places = pairs[2].shape[0]
    anywhere = pl.BlockSpec(memory_space=pl.ANY)
    return pl.pallas_call(
        functools.partial(tile_kernel, pieces=pieces, outs=len(outs), group=PAIRS_AT_ONCE, transpose=transpose),
        out_shape=[jax.ShapeDtypeStruct((rows, width), jnp.bfloat16) for rows in outs],
        in_specs=[pl.BlockSpec(memory_space=pltpu.SMEM)] * 4
        + [anywhere] * (1 + len(sources)),
        out_specs=[anywhere] * len(outs),
        scratch_shapes=[
            pltpu.VMEM((places, size, size), jnp.bfloat16),
            pltpu.VMEM((source_rows + size, width), jnp.bfloat16),
            pltpu.VMEM((sum_rows + size, width), jnp.float32),
        ]
        + [pltpu.VMEM((rows, width), jnp.bfloat16) for rows in outs]
        + [
            pltpu.SemaphoreType.DMA((places // (2 * PAIRS_AT_ONCE),)),
            pltpu.SemaphoreType.DMA((sum(blocks for blocks, _ in pieces),)),
            pltpu.SemaphoreType.DMA((len(outs),)),
        ],
        compiler_params=pltpu.CompilerParams(vmem_limit_bytes=(56 if transpose else 48) << 20),
        cost_estimate=pl.CostEstimate(
            flops=8 * slots * size * size * width,
            bytes_accessed=2 * slots * size * size + 4 * sum_rows * width,
            transcendentals=0,
        ),
    )(*pairs, block_tiles, *sources)


def exchange(chunks, axes):
    return lax.all_to_all(chunks, axes, 0, 0)


def spread(block, axes):
    devices = lax.axis_size(axes)
    return exchange(lax.optimization_barrier(jnp.broadcast_to(block[None], (devices,) + block.shape)), axes)


def add(*parts):
    return sum(part.astype(jnp.float32) for part in parts).astype(jnp.bfloat16)


def total(parts):
    return parts.astype(jnp.float32).sum(0)


def shift(block, axis, by):
    devices = lax.axis_size(axis)
    return lax.ppermute(block, axis, [(k, (k + by) % devices) for k in range(devices)])


def on_device(features, weight, tile_rows, tile_cols, tile_count, tile_values, grad_out):
    seg_rows, feat_width = features.shape
    block_tiles = tile_values[0, 0]
    size = block_tiles.shape[-1]
    live_count = tile_count[0, 0]
    tile_row_ids = tile_rows[0, 0]
    tile_col_ids = tile_cols[0, 0]
    far, near = lax.axis_size("row_far"), lax.axis_size("row_near")
    mid = lax.axis_size(("col_far", "col_mid"))
    row, col = ("row_far", "row_near"), ("col_far", "col_mid", "col_near")
    node_total = seg_rows * lax.axis_size(row) * lax.axis_size(col)
    seg_tiles = seg_rows // size
    far_rows, mid_rows = near * seg_rows, mid * seg_rows
    far_tiles = near * seg_tiles
    half_tiles, half_rows = far_tiles // 2, far_rows // 2

    away = (tile_col_ids // far_tiles - lax.axis_index("row_far")) % far
    inner = tile_col_ids % far_tiles
    upper = inner >= half_tiles
    col_take = jnp.where(away == 0, 0, jnp.where(away == 3, 1, away + 1)) * far_tiles + inner
    col_put = (
        jnp.where(
            away == 0,
            0,
            jnp.where(
                away == 1,
                jnp.where(upper, 1 * far_tiles, 3 * far_tiles),
                jnp.where(
                    away == 2,
                    jnp.where(upper, 2 * far_tiles, 1 * far_tiles),
                    jnp.where(upper, 3 * far_tiles, 2 * far_tiles),
                ),
            ),
        )
        + inner
    )
    other = (tile_row_ids // seg_tiles) % 2 != lax.axis_index("col_near")
    row_place = (
        other.astype(jnp.int32) * (mid * seg_tiles)
        + tile_row_ids // (2 * seg_tiles) * seg_tiles
        + tile_row_ids % seg_tiles
    )

    row_tiles, col_tiles = lax.axis_size(col) * seg_tiles, lax.axis_size(row) * seg_tiles
    row_pairs = pair_up(live_count, row_place, col_take, row_tiles, col_tiles)
    col_pairs = pair_up(live_count, col_put, row_place, col_tiles, row_tiles)

    own = lax.all_gather(features, "row_near", axis=0, tiled=True)
    left, right = shift(own, "row_far", 1), shift(own, "row_far", -1)
    low, high = shift(left[:half_rows], "row_far", 1), shift(right[half_rows:], "row_far", -1)
    keep, send = tile_products(
        row_pairs, block_tiles, [own, left, right, low, high], None, [mid_rows] * 2, False
    )
    paired = add(keep, shift(send, "col_near", 1))
    parts = exchange(paired.reshape(mid, seg_rows, feat_width), ("col_far", "col_mid"))
    aggregated = total(parts).astype(jnp.bfloat16)

    summed = jnp.dot(aggregated, weight, preferred_element_type=jnp.float32)
    activations, pullback = jax.vjp(gelu_tanh, summed)
    gradient = pullback(grad_out.astype(jnp.float32))[0].astype(jnp.bfloat16)
    activations = activations.astype(jnp.bfloat16)

    local_weight = lax.dot_general(
        aggregated, gradient, (((0,), (0,)), ((), ())), preferred_element_type=jnp.float32
    ).astype(jnp.bfloat16)
    load = jnp.concatenate(
        [
            jnp.broadcast_to(gradient[None], (mid,) + gradient.shape),
            local_weight.reshape(mid, -1, feat_width),
        ],
        axis=1,
    )
    mine = exchange(load, ("col_far", "col_mid"))
    theirs = shift(mine, "col_near", 1)
    weight_pair = total(mine[:, seg_rows:]) + total(theirs[:, seg_rows:])
    weight_rows = feat_width // lax.axis_size(col)
    weight_slice = lax.dynamic_slice_in_dim(weight_pair, lax.axis_index("col_near") * weight_rows, weight_rows, 0)
    weight_slice = weight_slice.astype(jnp.bfloat16)
    weight_slices = jnp.broadcast_to(weight_slice[None], (lax.axis_size(row),) + weight_slice.shape)
    mine, theirs, weight_slices = lax.optimization_barrier((mine, theirs, weight_slices))
    weight_slices = exchange(weight_slices, row)

    own, right_one, left_one, right_two, left_two = tile_products(
        col_pairs, block_tiles, [mine, theirs], seg_rows, [far_rows] * 3 + [half_rows] * 2, True
    )
    right_one, left_one, weight_slices = lax.optimization_barrier((right_one, left_one, weight_slices))
    from_left, from_right = shift(right_one, "row_far", 1), shift(left_one, "row_far", -1)
    weight_slice = total(weight_slices) * (1.0 / math.sqrt(node_total))
    weight_grad = spread(weight_slice.astype(jnp.bfloat16), col).reshape(feat_width, feat_width)
    from_left, from_right, weight_grad = lax.optimization_barrier((from_left, from_right, weight_grad))
    right_two, left_two = add(right_two, from_left[:half_rows]), add(left_two, from_right[half_rows:])
    low, high = shift(right_two, "row_far", 1), shift(left_two, "row_far", -1)
    low = add(own[:half_rows], low, from_right[:half_rows])
    high = add(own[half_rows:], high, from_left[half_rows:])
    mixed = jnp.concatenate([low, high], axis=0)
    parts = exchange(mixed.reshape(near, seg_rows, feat_width), "row_near")
    back_sum = total(parts).astype(jnp.bfloat16)

    feature_grad = lax.dot_general(
        back_sum, weight, (((1,), (1,)), ((), ())), preferred_element_type=jnp.float32
    ).astype(jnp.bfloat16)
    return (activations, feature_grad, weight_grad.astype(jnp.float32))


def solution(mesh):
    row, col = ("row_far", "row_near"), ("col_far", "col_mid", "col_near")
    split = Mesh(mesh.devices.reshape(4, 4, 4, 2, 2), row + col)
    by_row, by_col = P(row + col, None), P(col + row, None)
    placed = (
        by_col,
        P(),
        P(row, col, None),
        P(row, col, None),
        P(row, col),
        P(row, col, None, None, None),
        by_row,
    )
    return jax.shard_map(
        on_device,
        mesh=split,
        in_specs=placed,
        out_specs=(by_row, by_col, P()),
        check_vma=False,
    )
```
